512 devices in a mesh: expert: 64 (over z, y), tensor: 8 (over x, core).
Axes of the slice: x: 4, y: 8, z: 8, core: 2. Of those that a mesh axis runs over, the one named last changes fastest.
Arguments:
- tokens: bfloat16 [16384, 2048], P('expert', 'tensor'), may hold values from -6 to 6
- upstream: bfloat16 [16384, 2048], P('expert', 'tensor'), may hold values from -6 to 6
- expert_ids: int32 [16384, 1], P('expert'), may hold values from 0 to 63; in each aligned block of 256 rows (0 to 255, 256 to 511, ...) at most 8 rows name the same one
- w_gate: bfloat16 [64, 1408, 2048], P('expert', 'tensor'), may hold values from -0.125 to 0.125
- w_up: bfloat16 [64, 1408, 2048], P('expert', 'tensor'), may hold values from -0.125 to 0.125
- w_down: bfloat16 [64, 1408, 2048], P('expert', 'tensor'), may hold values from -0.15625 to 0.15625
Outputs:
- grad_tokens: bfloat16 [16384, 2048], P('expert', 'tensor')
- grad_gate: bfloat16 [64, 1408, 2048], P('expert', 'tensor')
- grad_up: bfloat16 [64, 1408, 2048], P('expert', 'tensor')
- grad_down: bfloat16 [64, 1408, 2048], P('expert', 'tensor')
The draws below stay inside these ranges and needn't reach their ends.
Inputs may be any that keep to these rules, and one draw needn't show every extreme that they name: `expert_ids`: among the 256 tokens of one index of expert, at most 8 name the same expert, and in some such block one expert is named exactly 8 times; every expert is named somewhere.
All inputs are finite; a program needn't handle non-finite values.
Results may differ from the reference program's by a relative error of at most 0.014.
Values may be sent and summed in bfloat16 or wider, within the bound.
A program may use at most 64 MiB of HBM per device.

```python
import math
import jax
import jax.numpy as jnp
import numpy as np
from jax import lax

D = 2048
FF = 1408
TOK_DEV = 256
EXPERTS = 64
CAP = 8
TOKENS = 16384


def level_of(rng, shape, shards, smallest, top_value):
    factor_of, own = 1.0, jax.random.fold_in(rng, 6)
    for dim, shards_of in shards:
        draws = jnp.exp(jax.random.uniform(jax.random.fold_in(own, dim), (shards_of,), jnp.float32, smallest / len(shards), top_value / len(shards)))
        factor_of = factor_of * jnp.repeat(draws, shape[dim] // shards_of).reshape([-1 if axis == dim else 1 for axis in range(len(shape))])
    return factor_of


def deal_out(own_key, own, number, rows, count, top, bound, slope):
    sequence = jax.random.permutation(own_key, count)
    crowded, ordinary = portions_of(count, rows * top, bound, slope, True), portions_of(count, rows * top, bound, slope, False)
    places = jnp.arange(count)

    def named(sizes, offset_by):
        used = int((sizes > 0).sum())
        fixed = max(1, used // 4)
        shifted = fixed + (places - fixed + offset_by * (used - fixed)) % max(1, count - fixed)
        return jnp.zeros((count,), jnp.int32).at[sequence[jnp.where(places < fixed, places, shifted)]].set(jnp.asarray(sizes, jnp.int32))

    sizes = jnp.where(number % 4 == 0, named(crowded, number // 4), named(ordinary, number - number // 4 - 1))
    mixed = jax.random.permutation(jax.random.fold_in(own, 3), count)
    giver, receiver = mixed[0:count // 2 * 2:2], mixed[1:count // 2 * 2:2]
    slack = jnp.minimum(sizes[giver] - 1, bound - sizes[receiver]) // 2
    slack = jnp.where((giver == sequence[0]) | (receiver == sequence[0]) | (sizes[receiver] == 0), 0, jnp.maximum(slack, 0))
    shifted = jax.random.randint(jax.random.fold_in(own, 4), (count // 2,), 0, 1 << 20) % (slack + 1)
    sizes = sizes.at[giver].add(-shifted).at[receiver].add(shifted)
    labels = jnp.searchsorted(jnp.cumsum(sizes), jnp.arange(rows * top), side="right").astype(jnp.int32)
    listing = labels.reshape(top, rows).T
    listing = listing[jax.random.permutation(jax.random.fold_in(own, 1), rows)]
    offset_by = jax.random.randint(jax.random.fold_in(own, 2), (rows, 1), 0, top)
    return jnp.take_along_axis(listing, (jnp.arange(top)[None, :] + offset_by) % top, axis=1)


def portions_of(amount, total, reach, slope, full):
    portions = [(1 << 20) // math.isqrt(standing ** slope) + 1 for standing in range(1, amount + 1)]
    largest = reach if full else min(reach, max(-(-total // amount), total * portions[0] // sum(portions)))
    least = 1 if total - largest >= amount - 1 else 0
    holding, surplus = [largest] + [least] * (amount - 1), total - largest - least * (amount - 1)
    while surplus > 0:
        movable = [i for i in range(1, amount) if holding[i] < largest] or [i for i in range(1, amount) if holding[i] < reach]
        whole, budget = sum([portions[i] for i in movable]), surplus
        for i in movable:
            extra = min(reach - holding[i], max(1, budget * portions[i] // whole), surplus)
            holding[i] = holding[i] + extra
            surplus = surplus - extra
    return np.array(holding)


def scatter_about(stream_key, shape, width, most, split=(), kind=jnp.bfloat16):
    entries = width * jax.random.normal(stream_key, shape, jnp.float32)
    if split:
        entries = entries * level_of(stream_key, shape, split, -0.22, 0.18)
    return jnp.clip(entries, -most, most).astype(kind)


def setup_inputs(seed: int = 0) -> dict:
    keys = jax.random.split(jax.random.key(seed), 7)
    tokens = scatter_about(keys[0], (TOKENS, D), 1.0, 6.0, ((0, 64), (1, 8)))
    upstream = scatter_about(keys[1], (TOKENS, D), 1.0, 6.0, ((0, 64), (1, 8)))
    expert_ids_keys = jax.random.split(jax.random.fold_in(keys[2], 1), TOKENS // TOK_DEV)
    expert_ids_turns = jax.random.permutation(jax.random.fold_in(keys[2], 3), TOKENS // TOK_DEV)
    expert_ids = jax.vmap(lambda own, number: deal_out(jax.random.fold_in(keys[2], 2), own, number, TOK_DEV, EXPERTS, 1, CAP, 2))(expert_ids_keys, expert_ids_turns).reshape((TOKENS, 1))
    w_gate = scatter_about(keys[3], (EXPERTS, FF, D), D ** -0.5, 0.125, ((0, 64), (1, 8)))
    w_up = scatter_about(keys[4], (EXPERTS, FF, D), D ** -0.5, 0.125, ((0, 64), (1, 8)))
    w_down = scatter_about(keys[5], (EXPERTS, FF, D), FF ** -0.5, 0.15625, ((0, 64), (1, 8)))
    return dict(tokens=tokens, upstream=upstream, expert_ids=expert_ids, w_gate=w_gate, w_up=w_up, w_down=w_down)


def reference(tokens, upstream, expert_ids, w_gate, w_up, w_down):
    route = expert_ids[:, 0]
    row_count = EXPERTS * CAP
    order_all = jnp.arange(TOKENS, dtype=jnp.int32)

    def one_expert(carry, items):
        expert_now, gate_rows, up_rows, down_rows = items
        sort_key = jnp.where(route == expert_now, 0, 1).astype(jnp.int32) * TOKENS + order_all
        picked = jnp.argsort(sort_key)[:row_count].astype(jnp.int32)
        valid = (route[picked] == expert_now)[:, None]
        x_rows = jnp.where(valid, tokens[picked], jnp.zeros((), jnp.bfloat16)).astype(jnp.bfloat16)
        dy_rows = jnp.where(valid, upstream[picked], jnp.zeros((), jnp.bfloat16)).astype(jnp.bfloat16)
        gate_pre = jnp.dot(x_rows, gate_rows.T, preferred_element_type=jnp.float32)
        up_pre = jnp.dot(x_rows, up_rows.T, preferred_element_type=jnp.float32)
        sig_gate = jax.nn.sigmoid(gate_pre)
        silu_gate = gate_pre * sig_gate
        hidden = (silu_gate * up_pre).astype(jnp.bfloat16)
        d_hidden = jnp.dot(dy_rows, down_rows.T, preferred_element_type=jnp.float32)
        d_up = (d_hidden * silu_gate).astype(jnp.bfloat16)
        d_gate = (d_hidden * up_pre * sig_gate * (1.0 + gate_pre * (1.0 - sig_gate))).astype(jnp.bfloat16)
        grad_down = jnp.dot(hidden.T, dy_rows, preferred_element_type=jnp.float32).astype(jnp.bfloat16)
        grad_gate = jnp.dot(d_gate.T, x_rows, preferred_element_type=jnp.float32).astype(jnp.bfloat16)
        grad_up = jnp.dot(d_up.T, x_rows, preferred_element_type=jnp.float32).astype(jnp.bfloat16)
        d_rows = jnp.dot(d_gate, gate_rows, preferred_element_type=jnp.float32) + jnp.dot(d_up, up_rows, preferred_element_type=jnp.float32)
        d_rows = jnp.where(valid, d_rows.astype(jnp.bfloat16), jnp.zeros((), jnp.bfloat16)).astype(jnp.bfloat16)
        carry = carry.at[picked].add(d_rows)
        return carry, (grad_gate, grad_up, grad_down)

    start = jnp.zeros((TOKENS, D), jnp.bfloat16)
    numbers = jnp.arange(EXPERTS, dtype=jnp.int32)
    grad_tokens, grads = lax.scan(one_expert, start, (numbers, w_gate, w_up, w_down))
    return (grad_tokens, grads[0], grads[1], grads[2])
```

```python
import jax
import jax.numpy as jnp
from jax import lax
from jax.sharding import PartitionSpec as P


def on_device(tokens, upstream, expert_ids, w_gate, w_up, w_down):
    experts = lax.axis_size("expert")
    tok_rows = tokens.shape[0]
    capacity = max(2, 2 * tok_rows // experts)
    slot_count = experts * capacity
    route = expert_ids[:, 0]
    onehot = (route[:, None] == jnp.arange(experts, dtype=jnp.int32)[None, :]).astype(jnp.int32)
    before = jnp.cumsum(onehot, axis=0) - onehot
    within = jnp.sum(before * onehot, axis=1)
    target = route * capacity + within
    placing = (target[None, :] == jnp.arange(slot_count, dtype=jnp.int32)[:, None]).astype(
        jnp.bfloat16
    )
    gate_rows = w_gate[0]
    up_rows = w_up[0]
    down_rows = w_down[0]

    feat = tokens.shape[1]
    own = jnp.concatenate([tokens, upstream], axis=1)
    placed = jnp.dot(placing, own, preferred_element_type=jnp.float32).astype(jnp.bfloat16)
    got = lax.all_to_all(
        placed.reshape(experts, capacity, 2 * feat), "expert", split_axis=0, concat_axis=0, tiled=True
    ).reshape(slot_count, 2 * feat)
    x_all = lax.all_gather(got[:, :feat], "tensor", axis=1, tiled=True)
    dy_all = lax.all_gather(got[:, feat:], "tensor", axis=1, tiled=True)
    gate_pre = lax.dot_general(
        x_all, gate_rows, (((1,), (1,)), ((), ())), preferred_element_type=jnp.float32
    )
    up_pre = lax.dot_general(
        x_all, up_rows, (((1,), (1,)), ((), ())), preferred_element_type=jnp.float32
    )
    gate_pre, up_pre = (gate_pre, up_pre)
    sig_gate = jax.nn.sigmoid(gate_pre)
    silu_gate = gate_pre * sig_gate
    hidden = (silu_gate * up_pre).astype(jnp.bfloat16)
    d_hidden = lax.dot_general(
        dy_all, down_rows, (((1,), (1,)), ((), ())), preferred_element_type=jnp.float32
    )
    block_grad = lax.dot_general(
        hidden, dy_all, (((0,), (0,)), ((), ())), preferred_element_type=jnp.float32
    )
    down_grad = block_grad
    d_hidden, down_grad = (d_hidden, down_grad)
    d_up = (d_hidden * silu_gate).astype(jnp.bfloat16)
    d_gate = (d_hidden * up_pre * sig_gate * (1.0 + gate_pre * (1.0 - sig_gate))).astype(
        jnp.bfloat16
    )
    grad_gate = lax.dot_general(
        d_gate, x_all, (((0,), (0,)), ((), ())), preferred_element_type=jnp.float32
    ).astype(jnp.bfloat16)
    grad_up = lax.dot_general(
        d_up, x_all, (((0,), (0,)), ((), ())), preferred_element_type=jnp.float32
    ).astype(jnp.bfloat16)
    grad_down = down_grad.astype(jnp.bfloat16)
    partial_rows = jnp.dot(d_gate, gate_rows, preferred_element_type=jnp.float32) + jnp.dot(
        d_up, up_rows, preferred_element_type=jnp.float32
    )
    totals = lax.psum_scatter(
        partial_rows.astype(jnp.bfloat16), "tensor", scatter_dimension=1, tiled=True
    )
    returned = lax.all_to_all(
        totals.reshape(experts, capacity, feat), "expert", split_axis=0, concat_axis=0, tiled=True
    ).reshape(slot_count, feat)
    grad_tokens = lax.dot_general(
        placing, returned, (((0,), (0,)), ((), ())), preferred_element_type=jnp.float32
    ).astype(jnp.bfloat16)
    return (grad_tokens, grad_gate[None], grad_up[None], grad_down[None])


def solution(mesh):
    in_specs = (
        P("expert", "tensor"),
        P("expert", "tensor"),
        P("expert", None),
        P("expert", "tensor", None),
        P("expert", "tensor", None),
        P("expert", "tensor", None),
    )
    out_specs = (
        P("expert", "tensor"),
        P("expert", "tensor", None),
        P("expert", "tensor", None),
        P("expert", "tensor", None),
    )
    return jax.shard_map(
        on_device, mesh=mesh, in_specs=in_specs, out_specs=out_specs, check_vma=False
    )
```

```python
import functools

import jax
import jax.numpy as jnp
from jax import lax
from jax.experimental import pallas as pl
from jax.experimental.pallas import tpu as pltpu
from jax.sharding import PartitionSpec as P

MESH = pl.DeviceIdType.MESH
F32 = jnp.float32
BF16 = jnp.bfloat16
CAP = 8
Y_SIDE = 8
CHUNKS = 4


def log2(value):
    return value.bit_length() - 1


def offset_of(place):
    odd = lax.rem(place, 2)
    return lax.div(place + 1, 2) * (2 * odd - 1)


def place_of(distance, side):
    return jnp.where(
        distance <= side // 2, jnp.maximum(2 * distance - 1, 0), 2 * (side - distance)
    )


def kernel(
    sizes,
    tok_ref,
    up_ref,
    ids_ref,
    wg_hbm,
    wu_hbm,
    wd_hbm,
    gt_ref,
    gg_ref,
    gu_ref,
    gd_ref,
    send,
    recv,
    gath,
    weights,
    grads,
    acts,
    part,
    sib_out,
    sib_in,
    half_out,
    half_in,
    full_out,
    full_in,
    ret_out,
    ret_in,
    w_sem,
    a2a_s,
    a2a_r,
    ag_s,
    ag_r,
    rs_s,
    rs_r,
    ret_s,
    ret_r,
    out_sem,
):
    zs, ys, xs, chunks = sizes
    experts = zs * ys
    rows_all = experts * CAP
    tok_rows, feat = tok_ref.shape
    blocks = experts // chunks
    rows = blocks * CAP
    half = rows // 2
    planes = zs // chunks
    hid = weights.shape[1]
    iters = chunks + 6

    e = lax.axis_index("expert")
    t = lax.axis_index("tensor")
    z, y = lax.div(e, ys), lax.rem(e, ys)
    x, c = lax.div(t, 2), lax.rem(t, 2)
    own = 2 * x + c
    right_x, left_x, far_x = lax.rem(x + 1, xs), lax.rem(x + xs - 1, xs), lax.rem(x + 2, xs)
    right, left, sib = (e, 2 * right_x + c), (e, 2 * left_x + c), (e, 2 * x + 1 - c)

    def peer(r, sign):
        dz, dy = offset_of(lax.div(r, ys)), offset_of(lax.rem(r, ys))
        pz, py = lax.rem(z + sign * dz + zs, zs), lax.rem(y + sign * dy + ys, ys)
        return (pz * ys + py, t)

    def remote(src, dst, ssem, rsem, device):
        return pltpu.make_async_remote_copy(
            src_ref=src,
            dst_ref=dst,
            send_sem=ssem,
            recv_sem=rsem,
            device_id=device,
            device_id_type=MESH,
        )

    barrier = pltpu.get_barrier_semaphore()

    def greet(r, carry):
        pl.semaphore_signal(barrier, inc=1, device_id=peer(r, 1), device_id_type=MESH)
        return carry

    for near in (right, left, sib):
        pl.semaphore_signal(barrier, inc=1, device_id=near, device_id_type=MESH)
    lax.fori_loop(1, experts, greet, 0)

    fetches = [
        pltpu.make_async_copy(w.at[0], weights.at[m], w_sem.at[m])
        for m, w in enumerate((wg_hbm, wu_hbm, wd_hbm))
    ]
    for fetch in fetches:
        fetch.start()

    ids = ids_ref[...]
    dz = (lax.shift_right_logical(ids, log2(ys)) - z) & (zs - 1)
    dy = ((ids & (ys - 1)) - y) & (ys - 1)
    rel = place_of(dz, zs) * ys + place_of(dy, ys)
    onehot = jnp.where(rel == lax.broadcasted_iota(jnp.int32, (tok_rows, experts), 1), 1.0, 0.0)
    row_i = lax.broadcasted_iota(jnp.int32, (tok_rows, tok_rows), 0)
    col_i = lax.broadcasted_iota(jnp.int32, (tok_rows, tok_rows), 1)
    earlier = jnp.where(col_i < row_i, 1.0, 0.0).astype(BF16)
    before = jnp.dot(earlier, onehot.astype(BF16), preferred_element_type=F32)
    within = jnp.sum(before * onehot, axis=1, keepdims=True)
    slot = rel.astype(F32) * float(CAP) + within
    slot_row = jnp.sum(jnp.where(row_i == col_i, slot, 0.0), axis=0, keepdims=True)
    slot_row = slot_row.astype(jnp.int32)
    slot_col = slot.astype(jnp.int32)
    placing = jnp.where(
        lax.broadcasted_iota(jnp.int32, (rows_all, tok_rows), 0) == slot_row, 1.0, 0.0
    ).astype(BF16)
    placed_x = jnp.dot(placing, tok_ref[...], preferred_element_type=F32)
    placed_d = jnp.dot(placing, up_ref[...], preferred_element_type=F32)
    send[:, 0:CAP, :] = placed_x.reshape(experts, CAP, feat).astype(BF16)
    send[:, CAP : 2 * CAP, :] = placed_d.reshape(experts, CAP, feat).astype(BF16)

    pl.semaphore_wait(barrier, experts - 1 + 3)

    def dispatch(r, carry):
        remote(
            send.at[r], recv.at[r], a2a_s, a2a_r.at[lax.div(r, blocks)], peer(r, 1)
        ).start()
        return carry

    pltpu.make_async_copy(send.at[0], recv.at[0], a2a_r.at[0]).start()
    lax.fori_loop(1, experts, dispatch, 0)

    def span(j):
        return pl.ds(pl.multiple_of(j * rows, rows), rows)

    def gather_copy(kind, j):
        s = span(j)
        left_b, right_b, far_b = 2 * left_x + c, 2 * right_x + c, 2 * far_x + c
        at, device = {
            0: (gath.at[own, :, s], right),
            1: (gath.at[own, :, s], left),
            2: (gath.at[left_b, 0, s], right),
            3: (gath.at[right_b, 1, s], left),
            4: (gath.at[own, :, s], sib),
            5: (gath.at[left_b, :, s], sib),
            6: (gath.at[right_b, :, s], sib),
            7: (gath.at[far_b, :, s], sib),
        }[kind]
        return remote(at, at, ag_s.at[kind, j], ag_r.at[kind, j], device)

    def gather_wait(kind, j):
        s = span(j)
        left_b, right_b, far_b = 2 * left_x + c, 2 * right_x + c, 2 * far_x + c
        o = 1 - 2 * c
        at, device = {
            0: (gath.at[left_b, :, s], right),
            1: (gath.at[right_b, :, s], left),
            2: (gath.at[far_b, 0, s], right),
            3: (gath.at[far_b, 1, s], left),
            4: (gath.at[own + o, :, s], sib),
            5: (gath.at[left_b + o, :, s], sib),
            6: (gath.at[right_b + o, :, s], sib),
            7: (gath.at[far_b + o, :, s], sib),
        }[kind]
        remote(at, at, ag_s.at[kind, j], ag_r.at[kind, j], device).wait_recv()

    def sum_copy(kind, j):
        src, dst, device = {
            0: (sib_out.at[j], sib_in.at[j], sib),
            1: (half_out.at[j, 0], half_in.at[j, 0], right),
            2: (half_out.at[j, 1], half_in.at[j, 1], left),
            3: (full_out.at[j, 0], full_in.at[j, 0], right),
            4: (full_out.at[j, 1], full_in.at[j, 1], left),
        }[kind]
        return remote(src, dst, rs_s.at[kind, j], rs_r.at[kind, j], device)

    def take_in(j):
        at = recv.at[pl.ds(j * blocks, blocks)]
        remote(at, at, a2a_s, a2a_r.at[j], sib).wait_recv()
        got = recv[pl.ds(j * blocks, blocks)].astype(F32)
        gath[own, 0, span(j), :] = got[:, 0:CAP, :].reshape(rows, feat).astype(BF16)
        gath[own, 1, span(j), :] = got[:, CAP : 2 * CAP, :].reshape(rows, feat).astype(BF16)
        for kind in (0, 1, 4):
            gather_copy(kind, j).start()

    def pass_near(j):
        gather_wait(0, j)
        gather_copy(2, j).start()
        gather_copy(5, j).start()
        gather_wait(1, j)
        gather_copy(3, j).start()
        gather_copy(6, j).start()

    def pass_far(j):
        gather_wait(2, j)
        gather_wait(3, j)
        gather_copy(7, j).start()

    def columns(b):
        return pl.ds(pl.multiple_of(b * feat, feat), feat)

    def multiply(j):
        for kind in (4, 5, 6, 7):
            gather_wait(kind, j)
        contract = (((1,), (1,)), ((), ()))
        gate = jnp.zeros((rows, hid), F32)
        up = jnp.zeros((rows, hid), F32)
        d_hidden = jnp.zeros((rows, hid), F32)
        for b in range(2 * xs):
            xb = gath[b, 0, span(j), :]
            db = gath[b, 1, span(j), :]
            at = slice(b * feat, (b + 1) * feat)
            gate += lax.dot_general(xb, weights[0, :, at], contract, preferred_element_type=F32)
            up += lax.dot_general(xb, weights[1, :, at], contract, preferred_element_type=F32)
            d_hidden += lax.dot_general(db, weights[2, :, at], contract, preferred_element_type=F32)
        sig = jax.nn.sigmoid(gate)
        silu = gate * sig
        hidden = (silu * up).astype(BF16)
        d_up = (d_hidden * silu).astype(BF16)
        d_gate = (d_hidden * up * sig * (1.0 + gate * (1.0 - sig))).astype(BF16)
        acts[0, span(j), :] = d_gate
        acts[1, span(j), :] = d_up
        acts[2, span(j), :] = hidden

        def rows_of(b):
            return jnp.dot(
                d_gate, weights[0, :, columns(b)], preferred_element_type=F32
            ) + jnp.dot(d_up, weights[1, :, columns(b)], preferred_element_type=F32)

        for k in range(xs):
            sib_out[j, k] = rows_of(2 * lax.rem(x + k, xs) + 1 - c).astype(BF16)
        sum_copy(0, j).start()
        for k in range(xs):
            part[j, k] = rows_of(2 * lax.rem(x + k, xs) + c)

    def sum_far(j):
        sum_copy(0, j).wait_recv()
        total = part[j, 2] + sib_in[j, 2].astype(F32)
        half_out[j, 0] = total[0:half].astype(BF16)
        half_out[j, 1] = total[half:rows].astype(BF16)
        sum_copy(1, j).start()
        sum_copy(2, j).start()

    def sum_near(j):
        to_right = part[j, 1] + sib_in[j, 1].astype(F32)
        to_left = part[j, 3] + sib_in[j, 3].astype(F32)
        sum_copy(1, j).wait_recv()
        full_out[j, 0, 0:half] = (to_right[0:half] + half_in[j, 0].astype(F32)).astype(BF16)
        full_out[j, 0, half:rows] = to_right[half:rows].astype(BF16)
        sum_copy(3, j).start()
        sum_copy(2, j).wait_recv()
        full_out[j, 1, 0:half] = to_left[0:half].astype(BF16)
        full_out[j, 1, half:rows] = (to_left[half:rows] + half_in[j, 1].astype(F32)).astype(BF16)
        sum_copy(4, j).start()

    def give_back(j):
        total = part[j, 0] + sib_in[j, 0].astype(F32)
        sum_copy(3, j).wait_recv()
        total += full_in[j, 0].astype(F32)
        sum_copy(4, j).wait_recv()
        total += full_in[j, 1].astype(F32)
        split = total.reshape(blocks, CAP, feat)
        ret_out[pl.ds(j * blocks, blocks), 0:CAP, :] = split[:, :, 0 : feat // 2].astype(BF16)
        ret_out[pl.ds(j * blocks, blocks), CAP : 2 * CAP, :] = split[:, :, feat // 2 :].astype(BF16)

        @pl.when(j == 0)
        def _():
            pltpu.make_async_copy(ret_out.at[0], ret_in.at[0], ret_r).start()

        def back(r, carry):
            remote(ret_out.at[r], ret_in.at[r], ret_s, ret_r, peer(r, -1)).start()
            return carry

        lax.fori_loop(jnp.maximum(j * blocks, 1), (j + 1) * blocks, back, 0)

    def step(i, carry):
        def stage(lag, work):
            @pl.when(jnp.logical_and(i >= lag, i < chunks + lag))
            def _():
                work(i - lag)

        stage(0, take_in)
        stage(1, pass_near)
        stage(2, pass_far)
        stage(6, give_back)
        stage(5, sum_near)
        stage(4, sum_far)

        @pl.when(i == 3)
        def _():
            for fetch in fetches:
                fetch.wait()

        stage(3, multiply)
        return carry

    lax.fori_loop(0, iters, step, 0)

    outs = (gg_ref, gu_ref, gd_ref)
    for m in range(3):
        turned = acts[m].T
        side = 1 if m == 2 else 0

        def column(b, carry):
            grads[m, :, columns(b)] = jnp.dot(
                turned, gath[b, side], preferred_element_type=F32
            ).astype(BF16)
            return carry

        lax.fori_loop(0, 2 * xs, column, 0)
        pltpu.make_async_copy(grads.at[m], outs[m].at[0], out_sem.at[m]).start()

    picking = jnp.where(
        lax.broadcasted_iota(jnp.int32, (tok_rows, rows_all), 1) == slot_col, 1.0, 0.0
    ).astype(BF16)
    remote(ret_in, ret_in, ret_s, ret_r, sib).wait_recv()
    back = ret_in[...].astype(F32)
    low = back[:, 0:CAP, :].reshape(rows_all, feat // 2).astype(BF16)
    high = back[:, CAP : 2 * CAP, :].reshape(rows_all, feat // 2).astype(BF16)
    gt_ref[:, 0 : feat // 2] = jnp.dot(picking, low, preferred_element_type=F32).astype(BF16)
    gt_ref[:, feat // 2 :] = jnp.dot(picking, high, preferred_element_type=F32).astype(BF16)

    rest = send.at[pl.ds(1, experts - 1)]
    remote(rest, rest, a2a_s, a2a_r.at[0], sib).wait_send()
    rest = ret_out.at[pl.ds(1, experts - 1)]
    remote(rest, rest, ret_s, ret_r, sib).wait_send()

    def drain(j, carry):
        for kind in range(8):
            gather_copy(kind, j).wait_send()
        for kind in range(5):
            sum_copy(kind, j).wait_send()
        return carry

    lax.fori_loop(0, chunks, drain, 0)
    for m in range(3):
        pltpu.make_async_copy(grads.at[m], outs[m].at[0], out_sem.at[m]).wait()


def on_device(tokens, upstream, expert_ids, w_gate, w_up, w_down):
    experts = lax.axis_size("expert")
    devices = lax.axis_size("tensor")
    ys = Y_SIDE
    zs, xs, chunks = experts // ys, devices // 2, CHUNKS
    tok_rows, feat = tokens.shape
    hid, width = w_gate.shape[1:]
    slots = experts * CAP
    rows = slots // chunks
    whole = pl.BlockSpec(memory_space=pltpu.VMEM)
    away = pl.BlockSpec(memory_space=pl.ANY)
    dma = pltpu.SemaphoreType.DMA
    return pl.pallas_call(
        functools.partial(kernel, (zs, ys, xs, chunks)),
        out_shape=(
            jax.ShapeDtypeStruct((tok_rows, feat), BF16),
            jax.ShapeDtypeStruct(w_gate.shape, BF16),
            jax.ShapeDtypeStruct(w_up.shape, BF16),
            jax.ShapeDtypeStruct(w_down.shape, BF16),
        ),
        in_specs=[whole, whole, whole, away, away, away],
        out_specs=(whole, away, away, away),
        scratch_shapes=[
            pltpu.VMEM((experts, 2 * CAP, feat), BF16),
            pltpu.VMEM((experts, 2 * CAP, feat), BF16),
            pltpu.VMEM((devices, 2, slots, feat), BF16),
            pltpu.VMEM((3, hid, width), BF16),
            pltpu.VMEM((3, hid, width), BF16),
            pltpu.VMEM((3, slots, hid), BF16),
            pltpu.VMEM((chunks, xs, rows, feat), F32),
            pltpu.VMEM((chunks, xs, rows, feat), BF16),
            pltpu.VMEM((chunks, xs, rows, feat), BF16),
            pltpu.VMEM((chunks, 2, rows // 2, feat), BF16),
            pltpu.VMEM((chunks, 2, rows // 2, feat), BF16),
            pltpu.VMEM((chunks, 2, rows, feat), BF16),
            pltpu.VMEM((chunks, 2, rows, feat), BF16),
            pltpu.VMEM((experts, 2 * CAP, feat // 2), BF16),
            pltpu.VMEM((experts, 2 * CAP, feat // 2), BF16),
            dma((3,)),
            dma,
            dma((chunks,)),
            dma((8, chunks)),
            dma((8, chunks)),
            dma((5, chunks)),
            dma((5, chunks)),
            dma,
            dma,
            dma((3,)),
        ],
        compiler_params=pltpu.CompilerParams(
            collective_id=0, has_side_effects=True, vmem_limit_bytes=48 * 1024 * 1024
        ),
    )(tokens, upstream, expert_ids, w_gate, w_up, w_down)


def solution(mesh):
    in_specs = (
        P("expert", "tensor"),
        P("expert", "tensor"),
        P("expert", None),
        P("expert", "tensor", None),
        P("expert", "tensor", None),
        P("expert", "tensor", None),
    )
    out_specs = (
        P("expert", "tensor"),
        P("expert", "tensor", None),
        P("expert", "tensor", None),
        P("expert", "tensor", None),
    )
    return jax.shard_map(
        on_device, mesh=mesh, in_specs=in_specs, out_specs=out_specs, check_vma=False
    )
```

```python
import functools

import jax
import jax.numpy as jnp
from jax import lax
from jax.experimental import pallas as pl
from jax.experimental.pallas import tpu as pltpu
from jax.sharding import PartitionSpec as P

MESH = pl.DeviceIdType.MESH
F32 = jnp.float32
BF16 = jnp.bfloat16
CAP = 8
Y_SIDE = 8
CHUNKS = 4
LAGS = (0, 1, 2, 3, 4, 5, 6)


def log2(value):
    return value.bit_length() - 1


def order_of(zs, ys, count):
    def far(pair):
        return min(pair[0], zs - pair[0]) + min(pair[1], ys - pair[1])

    pairs = sorted(((dz, dy) for dz in range(zs) for dy in range(ys)), key=far)
    ring = [pair for pair in pairs if 0 in pair]
    pairs = ring + [pair for pair in pairs if 0 not in pair]
    rest = pairs[count:]
    return pairs[:count] + rest[:count] + rest[2 * count :] + rest[count : 2 * count]


def kernel(
    sizes,
    tok_hbm,
    up_hbm,
    ids_hbm,
    wg_hbm,
    wu_hbm,
    wd_hbm,
    gt_ref,
    gg_ref,
    gu_ref,
    gd_ref,
    tok_ref,
    up_ref,
    ids_ref,
    send,
    recv,
    gath,
    weights,
    grads,
    acts,
    part,
    sib_out,
    sib_in,
    half_out,
    half_in,
    full_out,
    full_in,
    ret_out,
    ret_in,
    torus_sem,
    in_sem,
    w_sem,
    a2a_s,
    a2a_r,
    ag_s,
    ag_r,
    rs_s,
    rs_r,
    ret_s,
    ret_r,
    out_sem,
):
    zs, ys, xs, chunks = sizes
    experts = zs * ys
    rows_all = experts * CAP
    tok_rows, feat = tok_ref.shape
    blocks = experts // chunks
    rows = blocks * CAP
    half = rows // 2
    hid = weights.shape[1]
    iters = chunks + max(LAGS)

    e = lax.axis_index("expert")
    t = lax.axis_index("tensor")
    z, y = lax.div(e, ys), lax.rem(e, ys)
    x, c = lax.div(t, 2), lax.rem(t, 2)
    own = 2 * x + c
    right_x, left_x, far_x = lax.rem(x + 1, xs), lax.rem(x + xs - 1, xs), lax.rem(x + 2, xs)
    right, left, sib = (e, 2 * right_x + c), (e, 2 * left_x + c), (e, 2 * x + 1 - c)

    order = order_of(zs, ys, blocks)

    def moved(at, offset, side):
        to = at + offset % side
        return jnp.where(to >= side, to - side, to)

    to_z = [moved(z, o, zs) * ys for o in range(zs)]
    to_y = [moved(y, o, ys) for o in range(ys)]

    def peer(r, sign):
        dz, dy = order[r]
        return (to_z[sign * dz % zs] + to_y[sign * dy % ys], t)

    def remote(src, dst, ssem, rsem, device):
        return pltpu.make_async_remote_copy(
            src_ref=src,
            dst_ref=dst,
            send_sem=ssem,
            recv_sem=rsem,
            device_id=device,
            device_id_type=MESH,
        )

    barrier = pltpu.get_barrier_semaphore()

    for dz in range(1, zs):
        pl.semaphore_signal(barrier, inc=1, device_id=(to_z[dz] + y, t), device_id_type=MESH)
    for dy in range(1, ys):
        pl.semaphore_signal(barrier, inc=1, device_id=(z * ys + to_y[dy], t), device_id_type=MESH)
    early = [pair for pair in order[:blocks] if 0 not in pair]
    for dz, dy in early:
        device = (to_z[-dz % zs] + to_y[-dy % ys], t)
        pl.semaphore_signal(barrier, inc=1, device_id=device, device_id_type=MESH)
    for near in (right, left, sib):
        pl.semaphore_signal(barrier, inc=1, device_id=near, device_id_type=MESH)

    loads = [
        pltpu.make_async_copy(src, dst, in_sem.at[m])
        for m, (src, dst) in enumerate(((ids_hbm, ids_ref), (tok_hbm, tok_ref), (up_hbm, up_ref)))
    ]
    for load in loads:
        load.start()
    fetches = [
        pltpu.make_async_copy(w.at[0], weights.at[m], w_sem.at[m])
        for m, w in enumerate((wg_hbm, wu_hbm, wd_hbm))
    ]
    for fetch in fetches:
        fetch.start()

    expert_i = lax.broadcasted_iota(jnp.int32, (experts, 1), 0)
    place = sum(
        jnp.where(expert_i == dz * ys + dy, CAP * r, 0) for r, (dz, dy) in enumerate(order)
    ).astype(F32)
    row_i = lax.broadcasted_iota(jnp.int32, (tok_rows, tok_rows), 0)
    col_i = lax.broadcasted_iota(jnp.int32, (tok_rows, tok_rows), 1)
    earlier = jnp.where(row_i < col_i, 1.0, 0.0).astype(BF16)
    loads[0].wait()
    ids = ids_ref[...]
    dz = (lax.shift_right_logical(ids, log2(ys)) - z) & (zs - 1)
    dy = ((ids & (ys - 1)) - y) & (ys - 1)
    onehot = jnp.where(
        dz * ys + dy == lax.broadcasted_iota(jnp.int32, (experts, tok_rows), 0), 1.0, 0.0
    )
    before = jnp.dot(onehot.astype(BF16), earlier, preferred_element_type=F32)
    slot = jnp.sum(onehot * (before + place), axis=0, keepdims=True)
    slot_row = slot.astype(jnp.int32)

    pl.semaphore_wait(barrier, zs + ys - 2 + len(early) + 3)
    for dz in range(1, zs):
        pl.semaphore_signal(torus_sem, inc=1, device_id=(to_z[dz] + y, t), device_id_type=MESH)

    placing = jnp.where(
        lax.broadcasted_iota(jnp.int32, (rows_all, tok_rows), 0) == slot_row, 1.0, 0.0
    ).astype(BF16)
    loads[1].wait()
    loads[2].wait()
    placed_x = jnp.dot(placing, tok_ref[...], preferred_element_type=F32)
    placed_d = jnp.dot(placing, up_ref[...], preferred_element_type=F32)
    send[:, 0:CAP, :] = placed_x.reshape(experts, CAP, feat).astype(BF16)
    send[:, CAP : 2 * CAP, :] = placed_d.reshape(experts, CAP, feat).astype(BF16)


    pltpu.make_async_copy(send.at[0], recv.at[0], a2a_r.at[0]).start()
    for r in range(1, experts):
        if r == blocks:
            pl.semaphore_wait(torus_sem, zs - 1)
        remote(send.at[r], recv.at[r], a2a_s, a2a_r.at[r // blocks], peer(r, 1)).start()

    def span(j):
        return pl.ds(pl.multiple_of(j * rows, rows), rows)

    def gather_copy(kind, j):
        s = span(j)
        left_b, right_b, far_b = 2 * left_x + c, 2 * right_x + c, 2 * far_x + c
        at, device = {
            0: (gath.at[own, :, s], right),
            1: (gath.at[own, :, s], left),
            2: (gath.at[left_b, 0, s], right),
            3: (gath.at[right_b, 1, s], left),
            4: (gath.at[own, :, s], sib),
            5: (gath.at[left_b, :, s], sib),
            6: (gath.at[right_b, :, s], sib),
            7: (gath.at[far_b, :, s], sib),
        }[kind]
        return remote(at, at, ag_s.at[kind, j], ag_r.at[kind, j], device)

    def gather_wait(kind, j):
        s = span(j)
        left_b, right_b, far_b = 2 * left_x + c, 2 * right_x + c, 2 * far_x + c
        o = 1 - 2 * c
        at, device = {
            0: (gath.at[left_b, :, s], right),
            1: (gath.at[right_b, :, s], left),
            2: (gath.at[far_b, 0, s], right),
            3: (gath.at[far_b, 1, s], left),
            4: (gath.at[own + o, :, s], sib),
            5: (gath.at[left_b + o, :, s], sib),
            6: (gath.at[right_b + o, :, s], sib),
            7: (gath.at[far_b + o, :, s], sib),
        }[kind]
        remote(at, at, ag_s.at[kind, j], ag_r.at[kind, j], device).wait_recv()

    def sum_copy(kind, j):
        src, dst, device = {
            0: (sib_out.at[j], sib_in.at[j], sib),
            1: (half_out.at[j, 0], half_in.at[j, 0], right),
            2: (half_out.at[j, 1], half_in.at[j, 1], left),
            3: (full_out.at[j, 0], full_in.at[j, 0], right),
            4: (full_out.at[j, 1], full_in.at[j, 1], left),
        }[kind]
        return remote(src, dst, rs_s.at[kind, j], rs_r.at[kind, j], device)

    def take_in(j):
        at = recv.at[pl.ds(j * blocks, blocks)]
        remote(at, at, a2a_s, a2a_r.at[j], sib).wait_recv()
        got = recv[pl.ds(j * blocks, blocks)].astype(F32)
        gath[own, 0, span(j), :] = got[:, 0:CAP, :].reshape(rows, feat).astype(BF16)
        gath[own, 1, span(j), :] = got[:, CAP : 2 * CAP, :].reshape(rows, feat).astype(BF16)
        for kind in (0, 1, 4):
            gather_copy(kind, j).start()

    def pass_near(j):
        gather_wait(0, j)
        gather_copy(2, j).start()
        gather_copy(5, j).start()
        gather_wait(1, j)
        gather_copy(3, j).start()
        gather_copy(6, j).start()

    def pass_far(j):
        gather_wait(2, j)
        gather_wait(3, j)
        gather_copy(7, j).start()

    def columns(b):
        return pl.ds(pl.multiple_of(b * feat, feat), feat)

    def multiply(j):
        for kind in (4, 5, 6, 7):
            gather_wait(kind, j)
        contract = (((1,), (1,)), ((), ()))
        gate = jnp.zeros((rows, hid), F32)
        up = jnp.zeros((rows, hid), F32)
        d_hidden = jnp.zeros((rows, hid), F32)
        for b in range(2 * xs):
            xb = gath[b, 0, span(j), :]
            db = gath[b, 1, span(j), :]
            at = slice(b * feat, (b + 1) * feat)
            gate += lax.dot_general(xb, weights[0, :, at], contract, preferred_element_type=F32)
            up += lax.dot_general(xb, weights[1, :, at], contract, preferred_element_type=F32)
            d_hidden += lax.dot_general(db, weights[2, :, at], contract, preferred_element_type=F32)
        sig = jax.nn.sigmoid(gate)
        silu = gate * sig
        hidden = (silu * up).astype(BF16)
        d_up = (d_hidden * silu).astype(BF16)
        d_gate = (d_hidden * up * sig * (1.0 + gate * (1.0 - sig))).astype(BF16)
        acts[0, span(j), :] = d_gate
        acts[1, span(j), :] = d_up
        acts[2, span(j), :] = hidden

        def rows_of(b):
            return jnp.dot(
                d_gate, weights[0, :, columns(b)], preferred_element_type=F32
            ) + jnp.dot(d_up, weights[1, :, columns(b)], preferred_element_type=F32)

        for k in range(xs):
            sib_out[j, k] = rows_of(2 * lax.rem(x + k, xs) + 1 - c).astype(BF16)
        sum_copy(0, j).start()
        for k in range(xs):
            part[j, k] = rows_of(2 * lax.rem(x + k, xs) + c)

    def sum_far(j):
        sum_copy(0, j).wait_recv()
        total = part[j, 2] + sib_in[j, 2].astype(F32)
        half_out[j, 0] = total[0:half].astype(BF16)
        half_out[j, 1] = total[half:rows].astype(BF16)
        sum_copy(1, j).start()
        sum_copy(2, j).start()

    def sum_near(j):
        to_right = part[j, 1] + sib_in[j, 1].astype(F32)
        to_left = part[j, 3] + sib_in[j, 3].astype(F32)
        sum_copy(1, j).wait_recv()
        full_out[j, 0, 0:half] = (to_right[0:half] + half_in[j, 0].astype(F32)).astype(BF16)
        full_out[j, 0, half:rows] = to_right[half:rows].astype(BF16)
        sum_copy(3, j).start()
        sum_copy(2, j).wait_recv()
        full_out[j, 1, 0:half] = to_left[0:half].astype(BF16)
        full_out[j, 1, half:rows] = (to_left[half:rows] + half_in[j, 1].astype(F32)).astype(BF16)
        sum_copy(4, j).start()

    def give_back(j):
        total = part[j, 0] + sib_in[j, 0].astype(F32)
        sum_copy(3, j).wait_recv()
        total += full_in[j, 0].astype(F32)
        sum_copy(4, j).wait_recv()
        total += full_in[j, 1].astype(F32)
        split = total.reshape(blocks, CAP, feat)
        ret_out[pl.ds(j * blocks, blocks), 0:CAP, :] = split[:, :, 0 : feat // 2].astype(BF16)
        ret_out[pl.ds(j * blocks, blocks), CAP : 2 * CAP, :] = split[:, :, feat // 2 :].astype(BF16)

        for chunk in range(chunks):

            @pl.when(j == chunk)
            def _():
                for r in range(chunk * blocks, (chunk + 1) * blocks):
                    if r:
                        remote(ret_out.at[r], ret_in.at[r], ret_s, ret_r, peer(r, -1)).start()
                    else:
                        pltpu.make_async_copy(ret_out.at[0], ret_in.at[0], ret_r).start()

    def step(i, carry):
        def stage(lag, work):
            @pl.when(jnp.logical_and(i >= lag, i < chunks + lag))
            def _():
                work(i - lag)

        stage(LAGS[0], take_in)
        stage(LAGS[1], pass_near)
        stage(LAGS[2], pass_far)

        @pl.when(i == LAGS[3])
        def _():
            for fetch in fetches:
                fetch.wait()

        stage(LAGS[3], multiply)
        stage(LAGS[4], sum_far)
        stage(LAGS[5], sum_near)
        stage(LAGS[6], give_back)
        return carry

    lax.fori_loop(0, iters, step, 0)

    outs = (gg_ref, gu_ref, gd_ref)
    for m in range(3):
        turned = acts[m].T
        side = 1 if m == 2 else 0

        def column(b, carry):
            grads[m, :, columns(b)] = jnp.dot(
                turned, gath[b, side], preferred_element_type=F32
            ).astype(BF16)
            return carry

        lax.fori_loop(0, 2 * xs, column, 0)
        pltpu.make_async_copy(grads.at[m], outs[m].at[0], out_sem.at[m]).start()

    slot_col = jnp.sum(jnp.where(row_i == col_i, slot, 0.0), axis=1, keepdims=True)
    slot_col = slot_col.astype(jnp.int32)
    picking = jnp.where(
        lax.broadcasted_iota(jnp.int32, (tok_rows, rows_all), 1) == slot_col, 1.0, 0.0
    ).astype(BF16)
    remote(ret_in, ret_in, ret_s, ret_r, sib).wait_recv()
    back = ret_in[...].astype(F32)
    low = back[:, 0:CAP, :].reshape(rows_all, feat // 2).astype(BF16)
    high = back[:, CAP : 2 * CAP, :].reshape(rows_all, feat // 2).astype(BF16)
    gt_ref[:, 0 : feat // 2] = jnp.dot(picking, low, preferred_element_type=F32).astype(BF16)
    gt_ref[:, feat // 2 :] = jnp.dot(picking, high, preferred_element_type=F32).astype(BF16)

    rest = send.at[pl.ds(1, experts - 1)]
    remote(rest, rest, a2a_s, a2a_r.at[0], sib).wait_send()
    rest = ret_out.at[pl.ds(1, experts - 1)]
    remote(rest, rest, ret_s, ret_r, sib).wait_send()

    def drain(j, carry):
        for kind in range(8):
            gather_copy(kind, j).wait_send()
        for kind in range(5):
            sum_copy(kind, j).wait_send()
        return carry

    lax.fori_loop(0, chunks, drain, 0)
    for m in range(3):
        pltpu.make_async_copy(grads.at[m], outs[m].at[0], out_sem.at[m]).wait()


def on_device(tokens, upstream, expert_ids, w_gate, w_up, w_down):
    experts = lax.axis_size("expert")
    devices = lax.axis_size("tensor")
    ys = Y_SIDE
    zs, xs, chunks = experts // ys, devices // 2, CHUNKS
    tok_rows, feat = tokens.shape
    hid, width = w_gate.shape[1:]
    slots = experts * CAP
    rows = slots // chunks
    whole = pl.BlockSpec(memory_space=pltpu.VMEM)
    away = pl.BlockSpec(memory_space=pltpu.HBM)
    dma = pltpu.SemaphoreType.DMA
    hold = functools.partial(pltpu.with_memory_space_constraint, memory_space=pltpu.HBM)
    return pl.pallas_call(
        functools.partial(kernel, (zs, ys, xs, chunks)),
        out_shape=(
            jax.ShapeDtypeStruct((tok_rows, feat), BF16),
            jax.ShapeDtypeStruct(w_gate.shape, BF16),
            jax.ShapeDtypeStruct(w_up.shape, BF16),
            jax.ShapeDtypeStruct(w_down.shape, BF16),
        ),
        in_specs=[away] * 6,
        out_specs=(whole, away, away, away),
        scratch_shapes=[
            pltpu.VMEM(tokens.shape, BF16),
            pltpu.VMEM(upstream.shape, BF16),
            pltpu.VMEM((1, tok_rows), jnp.int32),
            pltpu.VMEM((experts, 2 * CAP, feat), BF16),
            pltpu.VMEM((experts, 2 * CAP, feat), BF16),
            pltpu.VMEM((devices, 2, slots, feat), BF16),
            pltpu.VMEM((3, hid, width), BF16),
            pltpu.VMEM((3, hid, width), BF16),
            pltpu.VMEM((3, slots, hid), BF16),
            pltpu.VMEM((chunks, xs, rows, feat), F32),
            pltpu.VMEM((chunks, xs, rows, feat), BF16),
            pltpu.VMEM((chunks, xs, rows, feat), BF16),
            pltpu.VMEM((chunks, 2, rows // 2, feat), BF16),
            pltpu.VMEM((chunks, 2, rows // 2, feat), BF16),
            pltpu.VMEM((chunks, 2, rows, feat), BF16),
            pltpu.VMEM((chunks, 2, rows, feat), BF16),
            pltpu.VMEM((experts, 2 * CAP, feat // 2), BF16),
            pltpu.VMEM((experts, 2 * CAP, feat // 2), BF16),
            pltpu.SemaphoreType.REGULAR,
            dma((3,)),
            dma((3,)),
            dma,
            dma((chunks,)),
            dma((8, chunks)),
            dma((8, chunks)),
            dma((5, chunks)),
            dma((5, chunks)),
            dma,
            dma,
            dma((3,)),
        ],
        compiler_params=pltpu.CompilerParams(
            collective_id=0, has_side_effects=True, vmem_limit_bytes=48 * 1024 * 1024
        ),
    )(
        hold(tokens),
        hold(upstream),
        hold(expert_ids.reshape(1, tok_rows)),
        hold(w_gate),
        hold(w_up),
        hold(w_down),
    )


def solution(mesh):
    in_specs = (
        P("expert", "tensor"),
        P("expert", "tensor"),
        P("expert", None),
        P("expert", "tensor", None),
        P("expert", "tensor", None),
        P("expert", "tensor", None),
    )
    out_specs = (
        P("expert", "tensor"),
        P("expert", "tensor", None),
        P("expert", "tensor", None),
        P("expert", "tensor", None),
    )
    return jax.shard_map(
        on_device, mesh=mesh, in_specs=in_specs, out_specs=out_specs, check_vma=False
    )
```

```python
import functools

import jax
import jax.numpy as jnp
from jax import lax
from jax.experimental import pallas as pl
from jax.experimental.pallas import tpu as pltpu
from jax.sharding import PartitionSpec as P

MESH = pl.DeviceIdType.MESH
F32 = jnp.float32
BF16 = jnp.bfloat16
CAP = 8
Y_SIDE = 8
CHUNKS = 4
LAGS = (0, 1, 2, 3, 4, 5, 7)


def log2(value):
    return value.bit_length() - 1


def order_of(zs, ys, count):
    def far(pair):
        return min(pair[0], zs - pair[0]) + min(pair[1], ys - pair[1])

    pairs = sorted(((dz, dy) for dz in range(zs) for dy in range(ys)), key=far)
    ring = [pair for pair in pairs if 0 in pair]
    pairs = ring + [pair for pair in pairs if 0 not in pair]
    return pairs


def kernel(
    sizes,
    tok_hbm,
    up_hbm,
    ids_hbm,
    wg_hbm,
    wu_hbm,
    wd_hbm,
    gt_ref,
    gg_ref,
    gu_ref,
    gd_ref,
    tok_ref,
    up_ref,
    ids_ref,
    send,
    recv,
    gath,
    weights,
    grads,
    acts,
    part,
    sib_out,
    sib_in,
    half_out,
    half_in,
    full_out,
    full_in,
    ret_out,
    ret_in,
    torus_sem,
    in_sem,
    w_sem,
    a2a_s,
    a2a_r,
    ag_s,
    ag_r,
    rs_s,
    rs_r,
    ret_s,
    ret_r,
    out_sem,
):
    zs, ys, xs, chunks = sizes
    experts = zs * ys
    rows_all = experts * CAP
    tok_rows, feat = tok_ref.shape
    blocks = experts // chunks
    rows = blocks * CAP
    half = rows // 2
    hid = weights.shape[1]
    iters = chunks + max(LAGS)

    e = lax.axis_index("expert")
    t = lax.axis_index("tensor")
    z, y = lax.div(e, ys), lax.rem(e, ys)
    x, c = lax.div(t, 2), lax.rem(t, 2)
    own = 2 * x + c
    right_x, left_x, far_x = lax.rem(x + 1, xs), lax.rem(x + xs - 1, xs), lax.rem(x + 2, xs)
    right, left, sib = (e, 2 * right_x + c), (e, 2 * left_x + c), (e, 2 * x + 1 - c)

    order = order_of(zs, ys, blocks)

    def moved(at, offset, side):
        to = at + offset % side
        return jnp.where(to >= side, to - side, to)

    to_z = [moved(z, o, zs) * ys for o in range(zs)]
    to_y = [moved(y, o, ys) for o in range(ys)]

    def peer(r, sign):
        dz, dy = order[r]
        return (to_z[sign * dz % zs] + to_y[sign * dy % ys], t)

    def remote(src, dst, ssem, rsem, device):
        return pltpu.make_async_remote_copy(
            src_ref=src,
            dst_ref=dst,
            send_sem=ssem,
            recv_sem=rsem,
            device_id=device,
            device_id_type=MESH,
        )

    barrier = pltpu.get_barrier_semaphore()

    for dz in range(1, zs):
        pl.semaphore_signal(barrier, inc=1, device_id=(to_z[dz] + y, t), device_id_type=MESH)
    for dy in range(1, ys):
        pl.semaphore_signal(barrier, inc=1, device_id=(z * ys + to_y[dy], t), device_id_type=MESH)
    early = [pair for pair in order[:blocks] if 0 not in pair]
    for dz, dy in early:
        device = (to_z[-dz % zs] + to_y[-dy % ys], t)
        pl.semaphore_signal(barrier, inc=1, device_id=device, device_id_type=MESH)
    for near in (right, left, sib):
        pl.semaphore_signal(barrier, inc=1, device_id=near, device_id_type=MESH)

    loads = [
        pltpu.make_async_copy(src, dst, in_sem.at[m])
        for m, (src, dst) in enumerate(((ids_hbm, ids_ref), (tok_hbm, tok_ref), (up_hbm, up_ref)))
    ]
    for load in loads:
        load.start()
    fetches = [
        pltpu.make_async_copy(w.at[0], weights.at[m], w_sem.at[m])
        for m, w in enumerate((wg_hbm, wu_hbm, wd_hbm))
    ]
    for fetch in fetches:
        fetch.start()

    expert_i = lax.broadcasted_iota(jnp.int32, (experts, 1), 0)
    place = sum(
        jnp.where(expert_i == dz * ys + dy, CAP * r, 0) for r, (dz, dy) in enumerate(order)
    ).astype(F32)
    row_i = lax.broadcasted_iota(jnp.int32, (tok_rows, tok_rows), 0)
    col_i = lax.broadcasted_iota(jnp.int32, (tok_rows, tok_rows), 1)
    earlier = jnp.where(row_i < col_i, 1.0, 0.0).astype(BF16)
    loads[0].wait()
    ids = ids_ref[...]
    dz = (lax.shift_right_logical(ids, log2(ys)) - z) & (zs - 1)
    dy = ((ids & (ys - 1)) - y) & (ys - 1)
    onehot = jnp.where(
        dz * ys + dy == lax.broadcasted_iota(jnp.int32, (experts, tok_rows), 0), 1.0, 0.0
    )
    before = jnp.dot(onehot.astype(BF16), earlier, preferred_element_type=F32)
    slot = jnp.sum(onehot * (before + place), axis=0, keepdims=True)
    slot_row = slot.astype(jnp.int32)

    pl.semaphore_wait(barrier, zs + ys - 2 + len(early) + 3)
    for dz in range(1, zs):
        pl.semaphore_signal(torus_sem, inc=1, device_id=(to_z[dz] + y, t), device_id_type=MESH)

    placing = jnp.where(
        lax.broadcasted_iota(jnp.int32, (rows_all, tok_rows), 0) == slot_row, 1.0, 0.0
    ).astype(BF16)
    loads[1].wait()
    loads[2].wait()
    placed_x = jnp.dot(placing, tok_ref[...], preferred_element_type=F32)
    placed_d = jnp.dot(placing, up_ref[...], preferred_element_type=F32)
    send[:, 0:CAP, :] = placed_x.reshape(experts, CAP, feat).astype(BF16)
    send[:, CAP : 2 * CAP, :] = placed_d.reshape(experts, CAP, feat).astype(BF16)


    pltpu.make_async_copy(send.at[0], recv.at[0], a2a_r.at[0]).start()
    def dispatch(chunk):
        for r in reversed(range(max(chunk * blocks, 1), (chunk + 1) * blocks)):
            remote(send.at[r], recv.at[r], a2a_s, a2a_r.at[chunk], peer(r, 1)).start()

    dispatch(0)
    pl.semaphore_wait(torus_sem, zs - 1)
    for chunk in range(1, chunks - 1):
        dispatch(chunk)

    def span(j):
        return pl.ds(pl.multiple_of(j * rows, rows), rows)

    def gather_copy(kind, j):
        s = span(j)
        left_b, right_b, far_b = 2 * left_x + c, 2 * right_x + c, 2 * far_x + c
        at, device = {
            0: (gath.at[own, :, s], right),
            1: (gath.at[own, :, s], left),
            2: (gath.at[left_b, 0, s], right),
            3: (gath.at[right_b, 1, s], left),
            4: (gath.at[own, :, s], sib),
            5: (gath.at[left_b, :, s], sib),
            6: (gath.at[right_b, :, s], sib),
            7: (gath.at[far_b, :, s], sib),
        }[kind]
        return remote(at, at, ag_s.at[kind, j], ag_r.at[kind, j], device)

    def gather_wait(kind, j):
        s = span(j)
        left_b, right_b, far_b = 2 * left_x + c, 2 * right_x + c, 2 * far_x + c
        o = 1 - 2 * c
        at, device = {
            0: (gath.at[left_b, :, s], right),
            1: (gath.at[right_b, :, s], left),
            2: (gath.at[far_b, 0, s], right),
            3: (gath.at[far_b, 1, s], left),
            4: (gath.at[own + o, :, s], sib),
            5: (gath.at[left_b + o, :, s], sib),
            6: (gath.at[right_b + o, :, s], sib),
            7: (gath.at[far_b + o, :, s], sib),
        }[kind]
        remote(at, at, ag_s.at[kind, j], ag_r.at[kind, j], device).wait_recv()

    def sum_copy(kind, j):
        src, dst, device = {
            0: (sib_out.at[j], sib_in.at[j], sib),
            1: (half_out.at[j, 0], half_in.at[j, 0], right),
            2: (half_out.at[j, 1], half_in.at[j, 1], left),
            3: (full_out.at[j, 0], full_in.at[j, 0], right),
            4: (full_out.at[j, 1], full_in.at[j, 1], left),
        }[kind]
        return remote(src, dst, rs_s.at[kind, j], rs_r.at[kind, j], device)

    def take_in(j):
        at = recv.at[pl.ds(j * blocks, blocks)]
        remote(at, at, a2a_s, a2a_r.at[j], sib).wait_recv()
        got = recv[pl.ds(j * blocks, blocks)].astype(F32)
        gath[own, 0, span(j), :] = got[:, 0:CAP, :].reshape(rows, feat).astype(BF16)
        gath[own, 1, span(j), :] = got[:, CAP : 2 * CAP, :].reshape(rows, feat).astype(BF16)
        for kind in (0, 1, 4):
            gather_copy(kind, j).start()

    def pass_near(j):
        gather_wait(0, j)
        gather_copy(2, j).start()
        gather_copy(5, j).start()
        gather_wait(1, j)
        gather_copy(3, j).start()
        gather_copy(6, j).start()

    def pass_far(j):
        gather_wait(2, j)
        gather_wait(3, j)
        gather_copy(7, j).start()

    def columns(b):
        return pl.ds(pl.multiple_of(b * feat, feat), feat)

    def multiply(j):
        for kind in (4, 5, 6, 7):
            gather_wait(kind, j)
        contract = (((1,), (1,)), ((), ()))
        gate = jnp.zeros((rows, hid), F32)
        up = jnp.zeros((rows, hid), F32)
        d_hidden = jnp.zeros((rows, hid), F32)
        for b in range(2 * xs):
            xb = gath[b, 0, span(j), :]
            db = gath[b, 1, span(j), :]
            at = slice(b * feat, (b + 1) * feat)
            gate += lax.dot_general(xb, weights[0, :, at], contract, preferred_element_type=F32)
            up += lax.dot_general(xb, weights[1, :, at], contract, preferred_element_type=F32)
            d_hidden += lax.dot_general(db, weights[2, :, at], contract, preferred_element_type=F32)
        sig = jax.nn.sigmoid(gate)
        silu = gate * sig
        hidden = (silu * up).astype(BF16)
        d_up = (d_hidden * silu).astype(BF16)
        d_gate = (d_hidden * up * sig * (1.0 + gate * (1.0 - sig))).astype(BF16)
        acts[0, span(j), :] = d_gate
        acts[1, span(j), :] = d_up
        acts[2, span(j), :] = hidden

        def rows_of(b):
            return jnp.dot(
                d_gate, weights[0, :, columns(b)], preferred_element_type=F32
            ) + jnp.dot(d_up, weights[1, :, columns(b)], preferred_element_type=F32)

        for k in range(xs):
            sib_out[j, k] = rows_of(2 * lax.rem(x + k, xs) + 1 - c).astype(BF16)
        sum_copy(0, j).start()
        for k in range(xs):
            part[j, k] = rows_of(2 * lax.rem(x + k, xs) + c)

    def sum_far(j):
        sum_copy(0, j).wait_recv()
        total = part[j, 2] + sib_in[j, 2].astype(F32)
        half_out[j, 0] = total[0:half].astype(BF16)
        half_out[j, 1] = total[half:rows].astype(BF16)
        sum_copy(1, j).start()
        sum_copy(2, j).start()

    def sum_near(j):
        to_right = part[j, 1] + sib_in[j, 1].astype(F32)
        to_left = part[j, 3] + sib_in[j, 3].astype(F32)
        sum_copy(1, j).wait_recv()
        full_out[j, 0, 0:half] = (to_right[0:half] + half_in[j, 0].astype(F32)).astype(BF16)
        full_out[j, 0, half:rows] = to_right[half:rows].astype(BF16)
        sum_copy(3, j).start()
        sum_copy(2, j).wait_recv()
        full_out[j, 1, 0:half] = to_left[0:half].astype(BF16)
        full_out[j, 1, half:rows] = (to_left[half:rows] + half_in[j, 1].astype(F32)).astype(BF16)
        sum_copy(4, j).start()

    def give_back(j):
        total = part[j, 0] + sib_in[j, 0].astype(F32)
        sum_copy(3, j).wait_recv()
        total += full_in[j, 0].astype(F32)
        sum_copy(4, j).wait_recv()
        total += full_in[j, 1].astype(F32)
        split = total.reshape(blocks, CAP, feat)
        ret_out[pl.ds(j * blocks, blocks), 0:CAP, :] = split[:, :, 0 : feat // 2].astype(BF16)
        ret_out[pl.ds(j * blocks, blocks), CAP : 2 * CAP, :] = split[:, :, feat // 2 :].astype(BF16)

        for chunk in range(chunks):

            @pl.when(j == chunk)
            def _():
                for r in reversed(range(chunk * blocks, (chunk + 1) * blocks)):
                    if r:
                        remote(ret_out.at[r], ret_in.at[r], ret_s, ret_r, peer(r, -1)).start()
                    else:
                        pltpu.make_async_copy(ret_out.at[0], ret_in.at[0], ret_r).start()

    outs = (gg_ref, gu_ref, gd_ref)

    def grad_copy(m):
        return pltpu.make_async_copy(grads.at[m], outs[m].at[0], out_sem.at[m])

    def grad(m):
        turned = acts[m].T
        side = 1 if m == 2 else 0

        def column(b, carry):
            grads[m, :, columns(b)] = jnp.dot(
                turned, gath[b, side], preferred_element_type=F32
            ).astype(BF16)
            return carry

        lax.fori_loop(0, 2 * xs, column, 0)
        grad_copy(m).start()

    def step(i, carry):
        def stage(lag, work, first=0):
            @pl.when(jnp.logical_and(i >= lag + first, i < chunks + lag))
            def _():
                work(i - lag)

        pl.when(i == 1)(functools.partial(pass_near, 0))
        stage(LAGS[0], take_in)
        pl.when(i == 1)(functools.partial(pass_far, 0))
        pl.when(i == 0)(functools.partial(dispatch, chunks - 1))
        stage(LAGS[1], pass_near, 1)
        stage(LAGS[2], pass_far, 1)

        @pl.when(i == LAGS[3])
        def _():
            for fetch in fetches:
                fetch.wait()

        stage(LAGS[3], multiply)
        stage(LAGS[4], sum_far)
        stage(LAGS[6], give_back)
        stage(LAGS[5], sum_near)
        return carry

    lax.fori_loop(0, iters, step, 0)

    for m in range(3):
        grad(m)
    slot_col = jnp.sum(jnp.where(row_i == col_i, slot, 0.0), axis=1, keepdims=True)
    slot_col = slot_col.astype(jnp.int32)
    picking = jnp.where(
        lax.broadcasted_iota(jnp.int32, (tok_rows, rows_all), 1) == slot_col, 1.0, 0.0
    ).astype(BF16)
    remote(ret_in, ret_in, ret_s, ret_r, sib).wait_recv()
    back = ret_in[...].astype(F32)
    low = back[:, 0:CAP, :].reshape(rows_all, feat // 2).astype(BF16)
    high = back[:, CAP : 2 * CAP, :].reshape(rows_all, feat // 2).astype(BF16)
    gt_ref[:, 0 : feat // 2] = jnp.dot(picking, low, preferred_element_type=F32).astype(BF16)
    gt_ref[:, feat // 2 :] = jnp.dot(picking, high, preferred_element_type=F32).astype(BF16)

    rest = send.at[pl.ds(1, experts - 1)]
    remote(rest, rest, a2a_s, a2a_r.at[0], sib).wait_send()
    rest = ret_out.at[pl.ds(1, experts - 1)]
    remote(rest, rest, ret_s, ret_r, sib).wait_send()

    def drain(j, carry):
        for kind in range(8):
            gather_copy(kind, j).wait_send()
        for kind in range(5):
            sum_copy(kind, j).wait_send()
        return carry

    lax.fori_loop(0, chunks, drain, 0)
    for m in range(3):
        grad_copy(m).wait()


def on_device(tokens, upstream, expert_ids, w_gate, w_up, w_down):
    experts = lax.axis_size("expert")
    devices = lax.axis_size("tensor")
    ys = Y_SIDE
    zs, xs, chunks = experts // ys, devices // 2, CHUNKS
    tok_rows, feat = tokens.shape
    hid, width = w_gate.shape[1:]
    slots = experts * CAP
    rows = slots // chunks
    whole = pl.BlockSpec(memory_space=pltpu.VMEM)
    away = pl.BlockSpec(memory_space=pltpu.HBM)
    dma = pltpu.SemaphoreType.DMA
    hold = functools.partial(pltpu.with_memory_space_constraint, memory_space=pltpu.HBM)
    return pl.pallas_call(
        functools.partial(kernel, (zs, ys, xs, chunks)),
        out_shape=(
            jax.ShapeDtypeStruct((tok_rows, feat), BF16),
            jax.ShapeDtypeStruct(w_gate.shape, BF16),
            jax.ShapeDtypeStruct(w_up.shape, BF16),
            jax.ShapeDtypeStruct(w_down.shape, BF16),
        ),
        in_specs=[away] * 6,
        out_specs=(whole, away, away, away),
        scratch_shapes=[
            pltpu.VMEM(tokens.shape, BF16),
            pltpu.VMEM(upstream.shape, BF16),
            pltpu.VMEM((1, tok_rows), jnp.int32),
            pltpu.VMEM((experts, 2 * CAP, feat), BF16),
            pltpu.VMEM((experts, 2 * CAP, feat), BF16),
            pltpu.VMEM((devices, 2, slots, feat), BF16),
            pltpu.VMEM((3, hid, width), BF16),
            pltpu.VMEM((3, hid, width), BF16),
            pltpu.VMEM((3, slots, hid), BF16),
            pltpu.VMEM((chunks, xs, rows, feat), F32),
            pltpu.VMEM((chunks, xs, rows, feat), BF16),
            pltpu.VMEM((chunks, xs, rows, feat), BF16),
            pltpu.VMEM((chunks, 2, rows // 2, feat), BF16),
            pltpu.VMEM((chunks, 2, rows // 2, feat), BF16),
            pltpu.VMEM((chunks, 2, rows, feat), BF16),
            pltpu.VMEM((chunks, 2, rows, feat), BF16),
            pltpu.VMEM((experts, 2 * CAP, feat // 2), BF16),
            pltpu.VMEM((experts, 2 * CAP, feat // 2), BF16),
            pltpu.SemaphoreType.REGULAR,
            dma((3,)),
            dma((3,)),
            dma,
            dma((chunks,)),
            dma((8, chunks)),
            dma((8, chunks)),
            dma((5, chunks)),
            dma((5, chunks)),
            dma,
            dma,
            dma((3,)),
        ],
        compiler_params=pltpu.CompilerParams(
            collective_id=0, has_side_effects=True, vmem_limit_bytes=48 * 1024 * 1024
        ),
    )(
        hold(tokens),
        hold(upstream),
        hold(expert_ids.reshape(1, tok_rows)),
        hold(w_gate),
        hold(w_up),
        hold(w_down),
    )


def solution(mesh):
    in_specs = (
        P("expert", "tensor"),
        P("expert", "tensor"),
        P("expert", None),
        P("expert", "tensor", None),
        P("expert", "tensor", None),
        P("expert", "tensor", None),
    )
    out_specs = (
        P("expert", "tensor"),
        P("expert", "tensor", None),
        P("expert", "tensor", None),
        P("expert", "tensor", None),
    )
    return jax.shard_map(
        on_device, mesh=mesh, in_specs=in_specs, out_specs=out_specs, check_vma=False
    )
```

```python
import functools

import jax
import jax.numpy as jnp
from jax import lax
from jax.experimental import pallas as pl
from jax.experimental.pallas import tpu as pltpu
from jax.sharding import PartitionSpec as P

MESH = pl.DeviceIdType.MESH
F32 = jnp.float32
BF16 = jnp.bfloat16
CAP = 8
Y_SIDE = 8
CHUNKS = 4
LAGS = (0, 1, 2, 3, 4, 5, 7)


def log2(value):
    return value.bit_length() - 1


def order_of(zs, ys, count):
    def far(pair):
        return min(pair[0], zs - pair[0]) + min(pair[1], ys - pair[1])

    pairs = sorted(((dz, dy) for dz in range(zs) for dy in range(ys)), key=far)
    ring = [pair for pair in pairs if 0 in pair]
    pairs = ring + [pair for pair in pairs if 0 not in pair]
    return pairs


def kernel(
    sizes,
    tok_hbm,
    up_hbm,
    ids_hbm,
    wg_hbm,
    wu_hbm,
    wd_hbm,
    gt_ref,
    gg_ref,
    gu_ref,
    gd_ref,
    tok_ref,
    up_ref,
    ids_ref,
    send,
    recv,
    gath,
    weights,
    grads,
    acts,
    part,
    sib_out,
    sib_in,
    half_out,
    half_in,
    full_out,
    full_in,
    ret_out,
    ret_in,
    torus_sem,
    in_sem,
    w_sem,
    a2a_s,
    a2a_r,
    ag_s,
    ag_r,
    rs_s,
    rs_r,
    ret_s,
    ret_r,
    out_sem,
):
    zs, ys, xs, chunks = sizes
    experts = zs * ys
    rows_all = experts * CAP
    tok_rows, feat = tok_ref.shape
    blocks = experts // chunks
    rows = blocks * CAP
    half = rows // 2
    hid = weights.shape[1]
    iters = chunks + max(LAGS)

    e = lax.axis_index("expert")
    t = lax.axis_index("tensor")
    z, y = lax.div(e, ys), lax.rem(e, ys)
    x, c = lax.div(t, 2), lax.rem(t, 2)
    own = 2 * x + c
    right_x, left_x, far_x = lax.rem(x + 1, xs), lax.rem(x + xs - 1, xs), lax.rem(x + 2, xs)
    right, left, sib = (e, 2 * right_x + c), (e, 2 * left_x + c), (e, 2 * x + 1 - c)

    order = order_of(zs, ys, blocks)

    def moved(at, offset, side):
        to = at + offset % side
        return jnp.where(to >= side, to - side, to)

    to_z = [moved(z, o, zs) * ys for o in range(zs)]
    to_y = [moved(y, o, ys) for o in range(ys)]

    def peer(r, sign):
        dz, dy = order[r]
        return (to_z[sign * dz % zs] + to_y[sign * dy % ys], t)

    def remote(src, dst, ssem, rsem, device):
        return pltpu.make_async_remote_copy(
            src_ref=src,
            dst_ref=dst,
            send_sem=ssem,
            recv_sem=rsem,
            device_id=device,
            device_id_type=MESH,
        )

    barrier = pltpu.get_barrier_semaphore()

    for dz in range(1, zs):
        pl.semaphore_signal(barrier, inc=1, device_id=(to_z[dz] + y, t), device_id_type=MESH)
    for dy in range(1, ys):
        pl.semaphore_signal(barrier, inc=1, device_id=(z * ys + to_y[dy], t), device_id_type=MESH)
    early = [pair for pair in order[:blocks] if 0 not in pair]
    for dz, dy in early:
        device = (to_z[-dz % zs] + to_y[-dy % ys], t)
        pl.semaphore_signal(barrier, inc=1, device_id=device, device_id_type=MESH)
    for near in (right, left, sib):
        pl.semaphore_signal(barrier, inc=1, device_id=near, device_id_type=MESH)

    loads = [
        pltpu.make_async_copy(src, dst, in_sem.at[m])
        for m, (src, dst) in enumerate(((ids_hbm, ids_ref), (tok_hbm, tok_ref), (up_hbm, up_ref)))
    ]
    for load in loads:
        load.start()
    fetches = [
        pltpu.make_async_copy(w.at[0], weights.at[m], w_sem.at[m])
        for m, w in enumerate((wg_hbm, wu_hbm, wd_hbm))
    ]
    for fetch in fetches:
        fetch.start()

    expert_i = lax.broadcasted_iota(jnp.int32, (experts, 1), 0)
    place = sum(
        jnp.where(expert_i == dz * ys + dy, CAP * r, 0) for r, (dz, dy) in enumerate(order)
    ).astype(F32)
    row_i = lax.broadcasted_iota(jnp.int32, (tok_rows, tok_rows), 0)
    col_i = lax.broadcasted_iota(jnp.int32, (tok_rows, tok_rows), 1)
    earlier = jnp.where(row_i < col_i, 1.0, 0.0).astype(BF16)
    loads[0].wait()
    ids = ids_ref[...]
    dz = (lax.shift_right_logical(ids, log2(ys)) - z) & (zs - 1)
    dy = ((ids & (ys - 1)) - y) & (ys - 1)
    onehot = jnp.where(
        dz * ys + dy == lax.broadcasted_iota(jnp.int32, (experts, tok_rows), 0), 1.0, 0.0
    )
    before = jnp.dot(onehot.astype(BF16), earlier, preferred_element_type=F32)
    slot = jnp.sum(onehot * (before + place), axis=0, keepdims=True)
    slot_row = slot.astype(jnp.int32)

    pl.semaphore_wait(barrier, zs + ys - 2 + len(early) + 3)
    for dz in range(1, zs):
        pl.semaphore_signal(torus_sem, inc=1, device_id=(to_z[dz] + y, t), device_id_type=MESH)

    placing = jnp.where(
        lax.broadcasted_iota(jnp.int32, (rows_all, tok_rows), 0) == slot_row, 1.0, 0.0
    ).astype(BF16)
    loads[1].wait()
    loads[2].wait()
    placed_x = jnp.dot(placing, tok_ref[...], preferred_element_type=F32)
    placed_d = jnp.dot(placing, up_ref[...], preferred_element_type=F32)
    send[:, 0:CAP, :] = placed_x.reshape(experts, CAP, feat).astype(BF16)
    send[:, CAP : 2 * CAP, :] = placed_d.reshape(experts, CAP, feat).astype(BF16)


    pltpu.make_async_copy(send.at[0], recv.at[0], a2a_r.at[0]).start()
    def dispatch(chunk):
        for r in reversed(range(max(chunk * blocks, 1), (chunk + 1) * blocks)):
            remote(send.at[r], recv.at[r], a2a_s, a2a_r.at[chunk], peer(r, 1)).start()

    dispatch(0)
    pl.semaphore_wait(torus_sem, zs - 1)
    for chunk in range(1, chunks - 1):
        dispatch(chunk)

    def span(j):
        return pl.ds(pl.multiple_of(j * rows, rows), rows)

    def gather_copy(kind, j):
        s = span(j)
        left_b, right_b, far_b = 2 * left_x + c, 2 * right_x + c, 2 * far_x + c
        at, device = {
            0: (gath.at[own, :, s], right),
            1: (gath.at[own, :, s], left),
            2: (gath.at[left_b, 0, s], right),
            3: (gath.at[right_b, 1, s], left),
            4: (gath.at[own, :, s], sib),
            5: (gath.at[left_b, :, s], sib),
            6: (gath.at[right_b, :, s], sib),
            7: (gath.at[far_b, :, s], sib),
        }[kind]
        return remote(at, at, ag_s.at[kind, j], ag_r.at[kind, j], device)

    def gather_wait(kind, j):
        s = span(j)
        left_b, right_b, far_b = 2 * left_x + c, 2 * right_x + c, 2 * far_x + c
        o = 1 - 2 * c
        at, device = {
            0: (gath.at[left_b, :, s], right),
            1: (gath.at[right_b, :, s], left),
            2: (gath.at[far_b, 0, s], right),
            3: (gath.at[far_b, 1, s], left),
            4: (gath.at[own + o, :, s], sib),
            5: (gath.at[left_b + o, :, s], sib),
            6: (gath.at[right_b + o, :, s], sib),
            7: (gath.at[far_b + o, :, s], sib),
        }[kind]
        remote(at, at, ag_s.at[kind, j], ag_r.at[kind, j], device).wait_recv()

    def sum_copy(kind, j):
        src, dst, device = {
            0: (sib_out.at[j], sib_in.at[j], sib),
            1: (half_out.at[j, 0], half_in.at[j, 0], right),
            2: (half_out.at[j, 1], half_in.at[j, 1], left),
            3: (full_out.at[j, 0], full_in.at[j, 0], right),
            4: (full_out.at[j, 1], full_in.at[j, 1], left),
        }[kind]
        return remote(src, dst, rs_s.at[kind, j], rs_r.at[kind, j], device)

    def take_in(j):
        at = recv.at[pl.ds(j * blocks, blocks)]
        remote(at, at, a2a_s, a2a_r.at[j], sib).wait_recv()
        got = recv[pl.ds(j * blocks, blocks)].astype(F32)
        gath[own, 0, span(j), :] = got[:, 0:CAP, :].reshape(rows, feat).astype(BF16)
        gath[own, 1, span(j), :] = got[:, CAP : 2 * CAP, :].reshape(rows, feat).astype(BF16)
        for kind in (0, 1, 4):
            gather_copy(kind, j).start()

    def pass_near(j):
        gather_wait(0, j)
        gather_copy(2, j).start()
        gather_copy(5, j).start()
        gather_wait(1, j)
        gather_copy(3, j).start()
        gather_copy(6, j).start()

    def pass_far(j):
        gather_wait(2, j)
        gather_wait(3, j)
        gather_copy(7, j).start()

    def columns(b):
        return pl.ds(pl.multiple_of(b * feat, feat), feat)

    def multiply(j):
        for kind in (4, 5, 6, 7):
            gather_wait(kind, j)
        contract = (((1,), (1,)), ((), ()))
        gate = jnp.zeros((rows, hid), F32)
        up = jnp.zeros((rows, hid), F32)
        d_hidden = jnp.zeros((rows, hid), F32)
        for b in range(2 * xs):
            xb = gath[b, 0, span(j), :]
            db = gath[b, 1, span(j), :]
            at = slice(b * feat, (b + 1) * feat)
            gate += lax.dot_general(xb, weights[0, :, at], contract, preferred_element_type=F32)
            up += lax.dot_general(xb, weights[1, :, at], contract, preferred_element_type=F32)
            d_hidden += lax.dot_general(db, weights[2, :, at], contract, preferred_element_type=F32)
        sig = jax.nn.sigmoid(gate)
        silu = gate * sig
        hidden = (silu * up).astype(BF16)
        d_up = (d_hidden * silu).astype(BF16)
        d_gate = (d_hidden * up * sig * (1.0 + gate * (1.0 - sig))).astype(BF16)
        acts[0, span(j), :] = d_gate
        acts[1, span(j), :] = d_up
        acts[2, span(j), :] = hidden

        def rows_of(b):
            return jnp.dot(
                d_gate, weights[0, :, columns(b)], preferred_element_type=F32
            ) + jnp.dot(d_up, weights[1, :, columns(b)], preferred_element_type=F32)

        for k in range(xs):
            sib_out[j, k] = rows_of(2 * lax.rem(x + k, xs) + 1 - c).astype(BF16)
        sum_copy(0, j).start()
        for k in range(xs):
            part[j, k] = rows_of(2 * lax.rem(x + k, xs) + c)

    def sum_far(j):
        sum_copy(0, j).wait_recv()
        total = part[j, 2] + sib_in[j, 2].astype(F32)
        half_out[j, 0] = total[0:half].astype(BF16)
        half_out[j, 1] = total[half:rows].astype(BF16)
        sum_copy(1, j).start()
        sum_copy(2, j).start()

    def sum_near(j):
        to_right = part[j, 1] + sib_in[j, 1].astype(F32)
        to_left = part[j, 3] + sib_in[j, 3].astype(F32)
        sum_copy(1, j).wait_recv()
        full_out[j, 0, 0:half] = (to_right[0:half] + half_in[j, 0].astype(F32)).astype(BF16)
        full_out[j, 0, half:rows] = to_right[half:rows].astype(BF16)
        sum_copy(3, j).start()
        sum_copy(2, j).wait_recv()
        full_out[j, 1, 0:half] = to_left[0:half].astype(BF16)
        full_out[j, 1, half:rows] = (to_left[half:rows] + half_in[j, 1].astype(F32)).astype(BF16)
        sum_copy(4, j).start()

    def give_back(j):
        total = part[j, 0] + sib_in[j, 0].astype(F32)
        sum_copy(3, j).wait_recv()
        total += full_in[j, 0].astype(F32)
        sum_copy(4, j).wait_recv()
        total += full_in[j, 1].astype(F32)
        split = total.reshape(blocks, CAP, feat)
        ret_out[pl.ds(j * blocks, blocks), 0:CAP, :] = split[:, :, 0 : feat // 2].astype(BF16)
        ret_out[pl.ds(j * blocks, blocks), CAP : 2 * CAP, :] = split[:, :, feat // 2 :].astype(BF16)

        for chunk in range(chunks):

            @pl.when(j == chunk)
            def _():
                for r in reversed(range(chunk * blocks, (chunk + 1) * blocks)):
                    if r:
                        remote(ret_out.at[r], ret_in.at[r], ret_s, ret_r, peer(r, -1)).start()
                    else:
                        pltpu.make_async_copy(ret_out.at[0], ret_in.at[0], ret_r).start()

    outs = (gg_ref, gu_ref, gd_ref)

    def grad_copy(m):
        return pltpu.make_async_copy(grads.at[m], outs[m].at[0], out_sem.at[m])

    def grad(m):
        turned = acts[m].T
        side = 1 if m == 2 else 0

        def column(b, carry):
            grads[m, :, columns(b)] = jnp.dot(
                turned, gath[b, side], preferred_element_type=F32
            ).astype(BF16)
            return carry

        lax.fori_loop(0, 2 * xs, column, 0)
        grad_copy(m).start()

    def step(i, carry):
        def stage(lag, work, first=0):
            @pl.when(jnp.logical_and(i >= lag + first, i < chunks + lag))
            def _():
                work(i - lag)

        pl.when(i == 1)(functools.partial(pass_near, 0))
        stage(LAGS[0], take_in)
        pl.when(i == 2)(functools.partial(pass_far, 0))
        pl.when(i == 0)(functools.partial(dispatch, chunks - 1))
        stage(LAGS[1], pass_near, 1)
        stage(LAGS[2], pass_far, 1)

        @pl.when(i == LAGS[3])
        def _():
            for fetch in fetches:
                fetch.wait()

        stage(LAGS[3], multiply)
        stage(LAGS[4], sum_far)
        stage(LAGS[6], give_back)
        stage(LAGS[5], sum_near)
        return carry

    lax.fori_loop(0, iters, step, 0)

    for m in range(3):
        grad(m)
    slot_col = jnp.sum(jnp.where(row_i == col_i, slot, 0.0), axis=1, keepdims=True)
    slot_col = slot_col.astype(jnp.int32)
    picking = jnp.where(
        lax.broadcasted_iota(jnp.int32, (tok_rows, rows_all), 1) == slot_col, 1.0, 0.0
    ).astype(BF16)
    remote(ret_in, ret_in, ret_s, ret_r, sib).wait_recv()
    back = ret_in[...].astype(F32)
    low = back[:, 0:CAP, :].reshape(rows_all, feat // 2).astype(BF16)
    high = back[:, CAP : 2 * CAP, :].reshape(rows_all, feat // 2).astype(BF16)
    gt_ref[:, 0 : feat // 2] = jnp.dot(picking, low, preferred_element_type=F32).astype(BF16)
    gt_ref[:, feat // 2 :] = jnp.dot(picking, high, preferred_element_type=F32).astype(BF16)

    rest = send.at[pl.ds(1, experts - 1)]
    remote(rest, rest, a2a_s, a2a_r.at[0], sib).wait_send()
    rest = ret_out.at[pl.ds(1, experts - 1)]
    remote(rest, rest, ret_s, ret_r, sib).wait_send()

    def drain(j, carry):
        for kind in range(8):
            gather_copy(kind, j).wait_send()
        for kind in range(5):
            sum_copy(kind, j).wait_send()
        return carry

    lax.fori_loop(0, chunks, drain, 0)
    for m in range(3):
        grad_copy(m).wait()


def on_device(tokens, upstream, expert_ids, w_gate, w_up, w_down):
    experts = lax.axis_size("expert")
    devices = lax.axis_size("tensor")
    ys = Y_SIDE
    zs, xs, chunks = experts // ys, devices // 2, CHUNKS
    tok_rows, feat = tokens.shape
    hid, width = w_gate.shape[1:]
    slots = experts * CAP
    rows = slots // chunks
    whole = pl.BlockSpec(memory_space=pltpu.VMEM)
    away = pl.BlockSpec(memory_space=pltpu.HBM)
    dma = pltpu.SemaphoreType.DMA
    hold = functools.partial(pltpu.with_memory_space_constraint, memory_space=pltpu.HBM)
    return pl.pallas_call(
        functools.partial(kernel, (zs, ys, xs, chunks)),
        out_shape=(
            jax.ShapeDtypeStruct((tok_rows, feat), BF16),
            jax.ShapeDtypeStruct(w_gate.shape, BF16),
            jax.ShapeDtypeStruct(w_up.shape, BF16),
            jax.ShapeDtypeStruct(w_down.shape, BF16),
        ),
        in_specs=[away] * 6,
        out_specs=(whole, away, away, away),
        scratch_shapes=[
            pltpu.VMEM(tokens.shape, BF16),
            pltpu.VMEM(upstream.shape, BF16),
            pltpu.VMEM((1, tok_rows), jnp.int32),
            pltpu.VMEM((experts, 2 * CAP, feat), BF16),
            pltpu.VMEM((experts, 2 * CAP, feat), BF16),
            pltpu.VMEM((devices, 2, slots, feat), BF16),
            pltpu.VMEM((3, hid, width), BF16),
            pltpu.VMEM((3, hid, width), BF16),
            pltpu.VMEM((3, slots, hid), BF16),
            pltpu.VMEM((chunks, xs, rows, feat), F32),
            pltpu.VMEM((chunks, xs, rows, feat), BF16),
            pltpu.VMEM((chunks, xs, rows, feat), BF16),
            pltpu.VMEM((chunks, 2, rows // 2, feat), BF16),
            pltpu.VMEM((chunks, 2, rows // 2, feat), BF16),
            pltpu.VMEM((chunks, 2, rows, feat), BF16),
            pltpu.VMEM((chunks, 2, rows, feat), BF16),
            pltpu.VMEM((experts, 2 * CAP, feat // 2), BF16),
            pltpu.VMEM((experts, 2 * CAP, feat // 2), BF16),
            pltpu.SemaphoreType.REGULAR,
            dma((3,)),
            dma((3,)),
            dma,
            dma((chunks,)),
            dma((8, chunks)),
            dma((8, chunks)),
            dma((5, chunks)),
            dma((5, chunks)),
            dma,
            dma,
            dma((3,)),
        ],
        compiler_params=pltpu.CompilerParams(
            collective_id=0, has_side_effects=True, vmem_limit_bytes=48 * 1024 * 1024
        ),
    )(
        hold(tokens),
        hold(upstream),
        hold(expert_ids.reshape(1, tok_rows)),
        hold(w_gate),
        hold(w_up),
        hold(w_down),
    )


def solution(mesh):
    in_specs = (
        P("expert", "tensor"),
        P("expert", "tensor"),
        P("expert", None),
        P("expert", "tensor", None),
        P("expert", "tensor", None),
        P("expert", "tensor", None),
    )
    out_specs = (
        P("expert", "tensor"),
        P("expert", "tensor", None),
        P("expert", "tensor", None),
        P("expert", "tensor", None),
    )
    return jax.shard_map(
        on_device, mesh=mesh, in_specs=in_specs, out_specs=out_specs, check_vma=False
    )
```
